32 devices in a mesh: segment: 4 (over y, core), row: 8 (over z, x).
Axes of the slice: x: 2, y: 2, z: 4, core: 2. Of those that a mesh axis runs over, the one named last changes fastest.
Arguments:
- snapshots: float32 [2048, 512], P('row', 'segment'), may hold values from -6 to 6
- basis: float32 [2048, 2048], P('row', 'segment'), may hold values from -0.125 to 0.125
Outputs:
- residual: float32 [2048, 512], P('row', 'segment')
- coefficients: float32 [2048, 512], P('segment')
- residual_rms: float32 [512], P('segment')
The draws below stay inside these ranges and needn't reach their ends.
All inputs are finite; a program needn't handle non-finite values.
Results may differ from the reference program's by a relative error of at most 0.0001.
Values sent between devices are 32-bit elements; how exact they have to be, the bound alone decides.
A program may use at most 64 MiB of HBM per device.

```python
import jax
import jax.numpy as jnp
from jax import lax

SEC = 512
TICKS = 2
BATCH = 128
ROWS = 2048
BASIS = 2048
COLS = 512


def steps_of(stream_key, dims, shards, least, largest):
    def one(position, shards_of):
        heights = jax.random.uniform(jax.random.fold_in(jax.random.fold_in(stream_key, 6), position), (shards_of,), jnp.float32, least / len(shards), largest / len(shards))
        return jnp.repeat(jnp.exp(heights), dims[position] // shards_of).reshape((-1,) + (1,) * (len(dims) - position - 1))

    factor_of = one(*shards[0])
    for cut in shards[1:]:
        factor_of = factor_of * one(*cut)
    return factor_of


def noise(key, dims, deviation, most, split=(), kind=jnp.bfloat16):
    values = jax.random.normal(key, dims, jnp.float32) * deviation
    if len(split) > 0:
        values = steps_of(key, dims, split, -0.22, 0.18) * values
    return jnp.clip(values, min=-most, max=most).astype(kind)


def setup_inputs(seed: int = 0) -> dict:
    keys = jax.random.split(jax.random.key(seed), 3)
    return {
        "snapshots": noise(keys[0], (ROWS, COLS), 1.0, 6.0, ((0, 8), (1, 4)), jnp.float32),
        "basis": noise(keys[1], (ROWS, BASIS), ROWS ** -0.5, 0.125, ((0, 8), (1, 4)), jnp.float32),
    }


def project(part, vec):
    high = lax.Precision.HIGHEST
    first = jnp.dot(part.T, vec, precision=high, preferred_element_type=jnp.float32)
    moved = vec - jnp.dot(part, first, precision=high, preferred_element_type=jnp.float32)
    second = jnp.dot(part.T, moved, precision=high, preferred_element_type=jnp.float32)
    return (moved - jnp.dot(part, second, precision=high, preferred_element_type=jnp.float32), first + second)

def reference(snapshots, basis):
    sections = basis.shape[1] // SEC

    def per_batch(batch_index, carry):
        resid, coeff = carry
        vec = lax.dynamic_slice_in_dim(snapshots, batch_index * BATCH, BATCH, 1)

        def per_section(step, inner):
            vec, coeff = inner
            section = (batch_index + step) % sections
            part = lax.dynamic_slice_in_dim(basis, section * SEC, SEC, 1)
            vec, coef = project(part, vec)
            coeff = lax.dynamic_update_slice(coeff, coef, (section * SEC, batch_index * BATCH))
            return (vec, coeff)
        vec, coeff = lax.fori_loop(jnp.int32(0), jnp.int32(TICKS), per_section, (vec, coeff))
        resid = lax.dynamic_update_slice(resid, vec, (jnp.int32(0), batch_index * BATCH))
        return (resid, coeff)
    resid = jnp.zeros(snapshots.shape, jnp.float32)
    coeff = jnp.zeros((basis.shape[1], snapshots.shape[1]), jnp.float32)
    resid, coeff = lax.fori_loop(jnp.int32(0), jnp.int32(sections), per_batch, (resid, coeff))
    rms = jnp.sqrt(lax.optimization_barrier(jnp.sum(resid * resid, axis=0)) / resid.shape[0])
    return (resid, coeff, rms)
```

```python
import functools

import jax
import jax.numpy as jnp
from jax import lax
from jax.experimental import pallas as pl
from jax.experimental.pallas import tpu as pltpu
from jax.sharding import PartitionSpec as P

TICKS = 2
MESH = pl.DeviceIdType.MESH
NN = (((1,), (0,)), ((), ()))
NT = (((1,), (1,)), ((), ()))


def split(x):
    high = x.astype(jnp.bfloat16)
    return high, (x - high.astype(jnp.float32)).astype(jnp.bfloat16)


def product(a, high_ref, low_ref, dims):
    rows = a.shape[0]
    high, low = split(a)
    both = lax.dot_general(
        jnp.concatenate([high, low], axis=0), high_ref[...], dims,
        preferred_element_type=jnp.float32,
    )
    rest = lax.dot_general(high, low_ref[...], dims, preferred_element_type=jnp.float32)
    return both[:rows] + (both[rows:] + rest)


def kernel(
    peers, sections, chunks, total_rows,
    v_ref, q_ref, res_ref, coef_ref, rms_ref,
    vt, qh, ql, q2, q2h, q2l, part, inbox, mine, full, csend, cin, ssend, sin,
    rs_send, rs_recv, ag_send, ag_recv, q_sem, c_send, c_recv, s_send, s_recv,
):
    row = lax.axis_index("row")
    seg = lax.axis_index("segment")
    after = lax.rem(seg + 1, sections)
    before = lax.rem(seg + sections - 1, sections)
    batch, sec = part.shape[1:]
    height = batch // chunks
    groups = height // 8
    blocks = peers // groups
    lanes = sec // blocks

    barrier = pltpu.get_barrier_semaphore()
    for k in range(1, peers):
        pl.semaphore_signal(
            barrier, inc=1, device_id={"row": lax.rem(row + k, peers)}, device_id_type=MESH
        )
    for other in (after, before):
        pl.semaphore_signal(barrier, inc=1, device_id={"segment": other}, device_id_type=MESH)

    def place(c, owner):
        top = pl.multiple_of(c * height + (owner // blocks) * 8, 8)
        left = pl.multiple_of(lax.rem(owner, blocks) * lanes, lanes)
        return pl.ds(top, 8), pl.ds(left, lanes)

    def take(p, c, sem):
        span = inbox.at[p, c, pl.ds(1, peers - 1)]
        pltpu.make_async_copy(span, span, sem).wait()

    high, low = split(q_ref[...])
    qh[...] = high
    ql[...] = low
    vt[...] = v_ref[...].T

    q_copy = pltpu.make_async_remote_copy(
        src_ref=q_ref, dst_ref=q2, send_sem=q_sem.at[0], recv_sem=q_sem.at[1],
        device_id={"segment": before}, device_id_type=MESH,
    )

    for p in range(2 * TICKS):
        now = (qh, ql) if p < 2 else (q2h, q2l)
        prior = (qh, ql) if p - 1 < 2 else (q2h, q2l)
        for c in range(chunks):
            span = pl.ds(c * height, height)
            if p > 0:
                take(p - 1, c, ag_recv.at[p - 1, c])
                vec = vt[span, :] - product(full[p - 1, span, :], *prior, NT)
                vt[span, :] = vec
            else:
                vec = vt[span, :]
            part[p, span, :] = product(vec, *now, NN)
            if p == 0 and c == 0:
                pl.semaphore_wait(barrier, peers + 1)
            for k in range(1, peers):
                peer = lax.rem(row + k, peers)
                pltpu.make_async_remote_copy(
                    src_ref=part.at[(p,) + place(c, peer)],
                    dst_ref=inbox.at[p, c, k],
                    send_sem=rs_send.at[p, c], recv_sem=rs_recv.at[p, c],
                    device_id={"row": peer}, device_id_type=MESH,
                ).start()
        if p == 0:
            q_copy.start()
            coef_ref[...] = jnp.zeros_like(coef_ref)
        if p == 2:
            coef_ref[:, pl.ds(pl.multiple_of(seg * batch, batch), batch)] = (
                full[0] + full[1]
            ).T
        for c in range(chunks):
            own = (p,) + place(c, row)
            take(p, c, rs_recv.at[p, c])
            total = part[own]
            for k in range(1, peers):
                total = total + inbox[p, c, k]
            mine[p, c] = total
            full[own] = total
            for k in range(1, peers):
                pltpu.make_async_remote_copy(
                    src_ref=mine.at[p, c], dst_ref=full.at[own],
                    send_sem=ag_send.at[p, c], recv_sem=ag_recv.at[p, c],
                    device_id={"row": lax.rem(row + k, peers)}, device_id_type=MESH,
                ).start()
        if p == 1:
            q_copy.wait()
            high, low = split(q2[...])
            q2h[...] = high
            q2l[...] = low

    moves = []
    for c in range(chunks):
        span = pl.ds(c * height, height)
        take(3, c, ag_recv.at[3, c])
        csend[span, :] = full[2, span, :] + full[3, span, :]
        move = pltpu.make_async_remote_copy(
            src_ref=csend.at[span], dst_ref=cin.at[span],
            send_sem=c_send.at[c], recv_sem=c_recv.at[c],
            device_id={"segment": after}, device_id_type=MESH,
        )
        move.start()
        moves.append(move)
        vt[span, :] = vt[span, :] - product(full[3, span, :], q2h, q2l, NT)
    res = vt[...].T
    sums = jnp.sum(res * res, axis=0, keepdims=True)
    ssend[...] = jnp.broadcast_to(sums, ssend.shape)
    for k in range(1, peers):
        pltpu.make_async_remote_copy(
            src_ref=ssend, dst_ref=sin.at[k], send_sem=s_send, recv_sem=s_recv,
            device_id={"row": lax.rem(row + k, peers)}, device_id_type=MESH,
        ).start()
    res_ref[...] = res
    for p in range(2 * TICKS):
        for c in range(chunks):
            take(p, c, rs_send.at[p, c])
            take(p, c, ag_send.at[p, c])
    for move in moves:
        move.wait()
    coef_ref[:, pl.ds(pl.multiple_of(before * batch, batch), batch)] = cin[...].T
    some = sin.at[pl.ds(1, peers - 1)]
    pltpu.make_async_copy(some, some, s_recv).wait()
    total = ssend[...]
    for k in range(1, peers):
        total = total + sin[k]
    rms_ref[...] = jnp.sqrt(total[:1] / total_rows)
    pltpu.make_async_copy(some, some, s_send).wait()


def per_device(snapshots, basis):
    sections = lax.axis_size("segment")
    peers = lax.axis_size("row")
    rows, batch = snapshots.shape
    sec = basis.shape[1]
    chunks = max(1, min(CHUNKS, batch * sec // (8 * 128 * peers)))
    height = batch // chunks
    lanes = sec // (peers // (height // 8))
    phases = 2 * TICKS
    f32, bf16 = jnp.float32, jnp.bfloat16
    vmem = pl.BlockSpec(memory_space=pltpu.VMEM)
    dma = pltpu.SemaphoreType.DMA
    res, coef, rms = pl.pallas_call(
        functools.partial(kernel, peers, sections, chunks, rows * peers),
        out_shape=(
            jax.ShapeDtypeStruct((rows, batch), f32),
            jax.ShapeDtypeStruct((sec, batch * sections), f32),
            jax.ShapeDtypeStruct((1, batch), f32),
        ),
        in_specs=[vmem, vmem],
        out_specs=(vmem, vmem, vmem),
        scratch_shapes=[
            pltpu.VMEM((batch, rows), f32),
            pltpu.VMEM((rows, sec), bf16),
            pltpu.VMEM((rows, sec), bf16),
            pltpu.VMEM((rows, sec), f32),
            pltpu.VMEM((rows, sec), bf16),
            pltpu.VMEM((rows, sec), bf16),
            pltpu.VMEM((phases, batch, sec), f32),
            pltpu.VMEM((phases, chunks, peers, 8, lanes), f32),
            pltpu.VMEM((phases, chunks, 8, lanes), f32),
            pltpu.VMEM((phases, batch, sec), f32),
            pltpu.VMEM((batch, sec), f32),
            pltpu.VMEM((batch, sec), f32),
            pltpu.VMEM((8, batch), f32),
            pltpu.VMEM((peers, 8, batch), f32),
            dma((phases, chunks)),
            dma((phases, chunks)),
            dma((phases, chunks)),
            dma((phases, chunks)),
            dma((2,)),
            dma((chunks,)),
            dma((chunks,)),
            dma,
            dma,
        ],
        compiler_params=pltpu.CompilerParams(collective_id=0, has_side_effects=True),
    )(snapshots, basis)
    return (res, coef, rms.reshape(batch))


CHUNKS = 4


def solution(mesh):
    placed = (P("row", "segment"), P("row", "segment"))
    return jax.shard_map(
        per_device,
        mesh=mesh,
        in_specs=placed,
        out_specs=(P("row", "segment"), P("segment", None), P("segment")),
        check_vma=False,
    )
```

```python
import functools

import jax
import jax.numpy as jnp
from jax import lax
from jax.experimental import pallas as pl
from jax.experimental.pallas import tpu as pltpu
from jax.sharding import PartitionSpec as P

TICKS = 2
MESH = pl.DeviceIdType.MESH
NN = (((1,), (0,)), ((), ()))
NT = (((1,), (1,)), ((), ()))


def split(x):
    high = x.astype(jnp.bfloat16)
    return high, (x - high.astype(jnp.float32)).astype(jnp.bfloat16)


def product(a, high_ref, low_ref, dims):
    rows = a.shape[0]
    high, low = split(a)
    both = lax.dot_general(
        jnp.concatenate([high, low], axis=0), high_ref[...], dims,
        preferred_element_type=jnp.float32,
    )
    rest = lax.dot_general(high, low_ref[...], dims, preferred_element_type=jnp.float32)
    return both[:rows] + (both[rows:] + rest)


def kernel(
    peers, sections, chunks,
    v_hbm, q_hbm, res_ref, here_ref, there_ref, sums_ref,
    v_ref, q_ref, in_sem,
    vt, qh, ql, q2, q2h, q2l, part, inbox, mine, full, csend, cin, ssend, sin,
    rs_send, rs_recv, ag_send, ag_recv, q_sem, c_send, c_recv, s_send, s_recv,
):
    q_load = pltpu.make_async_copy(q_hbm, q_ref, in_sem.at[0])
    v_load = pltpu.make_async_copy(v_hbm, v_ref, in_sem.at[1])
    q_load.start()
    v_load.start()
    row = lax.axis_index("row")
    seg = lax.axis_index("segment")
    after = lax.rem(seg + 1, sections)
    before = lax.rem(seg + sections - 1, sections)
    batch, sec = part.shape[1:]
    height = batch // chunks
    groups = height // 8
    blocks = peers // groups
    lanes = sec // blocks

    barrier = pltpu.get_barrier_semaphore()
    for k in range(1, peers):
        pl.semaphore_signal(
            barrier, inc=1, device_id={"row": lax.rem(row + k, peers)}, device_id_type=MESH
        )
    for other in (after, before):
        pl.semaphore_signal(barrier, inc=1, device_id={"segment": other}, device_id_type=MESH)

    def place(c, owner):
        top = pl.multiple_of(c * height + (owner // blocks) * 8, 8)
        left = pl.multiple_of(lax.rem(owner, blocks) * lanes, lanes)
        return pl.ds(top, 8), pl.ds(left, lanes)

    def take(p, c, sem):
        span = inbox.at[p, c, pl.ds(1, peers - 1)]
        pltpu.make_async_copy(span, span, sem).wait()

    v_load.wait()
    vt[...] = v_ref[...].T
    q_load.wait()
    high, low = split(q_ref[...])
    qh[...] = high
    ql[...] = low

    q_copy = pltpu.make_async_remote_copy(
        src_ref=q_ref, dst_ref=q2, send_sem=q_sem.at[0], recv_sem=q_sem.at[1],
        device_id={"segment": before}, device_id_type=MESH,
    )

    for p in range(2 * TICKS):
        now = (qh, ql) if p < 2 else (q2h, q2l)
        prior = (qh, ql) if p - 1 < 2 else (q2h, q2l)
        for c in range(chunks):
            span = pl.ds(c * height, height)
            if p > 0:
                take(p - 1, c, ag_recv.at[p - 1, c])
                vec = vt[span, :] - product(full[p - 1, span, :], *prior, NT)
                vt[span, :] = vec
            else:
                vec = vt[span, :]
            part[p, span, :] = product(vec, *now, NN)
            if p == 0 and c == 0:
                pl.semaphore_wait(barrier, peers + 1)
            for k in range(1, peers):
                peer = lax.rem(row + k, peers)
                pltpu.make_async_remote_copy(
                    src_ref=part.at[(p,) + place(c, peer)],
                    dst_ref=inbox.at[p, c, k],
                    send_sem=rs_send.at[p, c], recv_sem=rs_recv.at[p, c],
                    device_id={"row": peer}, device_id_type=MESH,
                ).start()
        if p == 0:
            q_copy.start()
        if p == 2:
            here_ref[...] = (full[0] + full[1]).T
        for c in range(chunks):
            own = (p,) + place(c, row)
            take(p, c, rs_recv.at[p, c])
            total = part[own]
            for k in range(1, peers):
                total = total + inbox[p, c, k]
            mine[p, c] = total
            full[own] = total
            for k in range(1, peers):
                pltpu.make_async_remote_copy(
                    src_ref=mine.at[p, c], dst_ref=full.at[own],
                    send_sem=ag_send.at[p, c], recv_sem=ag_recv.at[p, c],
                    device_id={"row": lax.rem(row + k, peers)}, device_id_type=MESH,
                ).start()
        if p == 1:
            q_copy.wait()
            high, low = split(q2[...])
            q2h[...] = high
            q2l[...] = low

    moves = []
    for c in range(chunks):
        span = pl.ds(c * height, height)
        take(3, c, ag_recv.at[3, c])
        csend[span, :] = full[2, span, :] + full[3, span, :]
        move = pltpu.make_async_remote_copy(
            src_ref=csend.at[span], dst_ref=cin.at[span],
            send_sem=c_send.at[c], recv_sem=c_recv.at[c],
            device_id={"segment": after}, device_id_type=MESH,
        )
        move.start()
        moves.append(move)
        vt[span, :] = vt[span, :] - product(full[3, span, :], q2h, q2l, NT)
    res = vt[...].T
    sums = jnp.sum(res * res, axis=0, keepdims=True)
    ssend[...] = jnp.broadcast_to(sums, ssend.shape)
    for k in range(1, peers):
        pltpu.make_async_remote_copy(
            src_ref=ssend, dst_ref=sin.at[k], send_sem=s_send, recv_sem=s_recv,
            device_id={"row": lax.rem(row + k, peers)}, device_id_type=MESH,
        ).start()
    res_ref[...] = res
    for p in range(2 * TICKS):
        for c in range(chunks):
            take(p, c, rs_send.at[p, c])
            take(p, c, ag_send.at[p, c])
    for move in moves:
        move.wait()
    there_ref[...] = cin[...].T
    some = sin.at[pl.ds(1, peers - 1)]
    pltpu.make_async_copy(some, some, s_recv).wait()
    total = ssend[...]
    for k in range(1, peers):
        total = total + sin[k]
    sums_ref[...] = total
    pltpu.make_async_copy(some, some, s_send).wait()


def finish(sections, total_rows, res_ref, here_ref, there_ref, sums_ref, out_ref, coef_ref, rms_ref):
    seg = lax.axis_index("segment")
    batch = here_ref.shape[1]
    out_ref[...] = res_ref[...]
    rms_ref[...] = jnp.sqrt(sums_ref[...][:1] / total_rows)
    coef_ref[...] = jnp.zeros_like(coef_ref)
    before = lax.rem(seg + sections - 1, sections)
    coef_ref[:, pl.ds(pl.multiple_of(seg * batch, batch), batch)] = here_ref[...]
    coef_ref[:, pl.ds(pl.multiple_of(before * batch, batch), batch)] = there_ref[...]


def per_device(snapshots, basis):
    sections = lax.axis_size("segment")
    peers = lax.axis_size("row")
    rows, batch = snapshots.shape
    sec = basis.shape[1]
    chunks = max(1, min(CHUNKS, batch * sec // (8 * 128 * peers)))
    height = batch // chunks
    lanes = sec // (peers // (height // 8))
    phases = 2 * TICKS
    f32, bf16 = jnp.float32, jnp.bfloat16
    vmem = pl.BlockSpec(memory_space=pltpu.VMEM)
    dma = pltpu.SemaphoreType.DMA
    anywhere = pl.BlockSpec(memory_space=pl.ANY)
    parts = pl.pallas_call(
        functools.partial(kernel, peers, sections, chunks),
        out_shape=(
            jax.ShapeDtypeStruct((rows, batch), f32),
            jax.ShapeDtypeStruct((sec, batch), f32),
            jax.ShapeDtypeStruct((sec, batch), f32),
            jax.ShapeDtypeStruct((8, batch), f32),
        ),
        in_specs=[anywhere, anywhere],
        out_specs=(vmem, vmem, vmem, vmem),
        scratch_shapes=[
            pltpu.VMEM((rows, batch), f32),
            pltpu.VMEM((rows, sec), f32),
            dma((2,)),
            pltpu.VMEM((batch, rows), f32),
            pltpu.VMEM((rows, sec), bf16),
            pltpu.VMEM((rows, sec), bf16),
            pltpu.VMEM((rows, sec), f32),
            pltpu.VMEM((rows, sec), bf16),
            pltpu.VMEM((rows, sec), bf16),
            pltpu.VMEM((phases, batch, sec), f32),
            pltpu.VMEM((phases, chunks, peers, 8, lanes), f32),
            pltpu.VMEM((phases, chunks, 8, lanes), f32),
            pltpu.VMEM((phases, batch, sec), f32),
            pltpu.VMEM((batch, sec), f32),
            pltpu.VMEM((batch, sec), f32),
            pltpu.VMEM((8, batch), f32),
            pltpu.VMEM((peers, 8, batch), f32),
            dma((phases, chunks)),
            dma((phases, chunks)),
            dma((phases, chunks)),
            dma((phases, chunks)),
            dma((2,)),
            dma((chunks,)),
            dma((chunks,)),
            dma,
            dma,
        ],
        compiler_params=pltpu.CompilerParams(collective_id=0, has_side_effects=True),
    )(snapshots, basis)
    res, coef, rms = pl.pallas_call(
        functools.partial(finish, sections, rows * peers),
        out_shape=(
            jax.ShapeDtypeStruct((rows, batch), f32),
            jax.ShapeDtypeStruct((sec, batch * sections), f32),
            jax.ShapeDtypeStruct((1, batch), f32),
        ),
        in_specs=[vmem] * 4,
        out_specs=(vmem, vmem, vmem),
    )(*parts)
    return (res, coef, rms.reshape(batch))


CHUNKS = 4


def solution(mesh):
    placed = (P("row", "segment"), P("row", "segment"))
    return jax.shard_map(
        per_device,
        mesh=mesh,
        in_specs=placed,
        out_specs=(P("row", "segment"), P("segment", None), P("segment")),
        check_vma=False,
    )
```

```python
import functools

import jax
import jax.numpy as jnp
from jax import lax
from jax.experimental import pallas as pl
from jax.experimental.pallas import tpu as pltpu
from jax.sharding import PartitionSpec as P

TICKS = 2
MESH = pl.DeviceIdType.MESH
NN = (((1,), (0,)), ((), ()))
NT = (((1,), (1,)), ((), ()))


def split(x):
    high = x.astype(jnp.bfloat16)
    return high, (x - high.astype(jnp.float32)).astype(jnp.bfloat16)


def product(a, high_ref, low_ref, dims):
    rows = a.shape[0]
    high, low = split(a)
    both = lax.dot_general(
        jnp.concatenate([high, low], axis=0), high_ref[...], dims,
        preferred_element_type=jnp.float32,
    )
    rest = lax.dot_general(high, low_ref[...], dims, preferred_element_type=jnp.float32)
    return both[:rows] + (both[rows:] + rest)


def kernel(
    peers, sections, chunks,
    v_hbm, q_hbm, res_ref, here_ref, there_ref, sums_ref,
    v_ref, q_ref, in_sem,
    vt, qh, ql, q2, q2h, q2l, part, inbox, mine, full, csend, cin, ssend, sin,
    rs_send, rs_recv, ag_send, ag_recv, q_sem, c_send, c_recv, s_send, s_recv,
):
    q_load = pltpu.make_async_copy(q_hbm, q_ref, in_sem.at[0])
    v_load = pltpu.make_async_copy(v_hbm, v_ref, in_sem.at[1])
    q_load.start()
    v_load.start()
    row = lax.axis_index("row")
    seg = lax.axis_index("segment")
    after = lax.rem(seg + 1, sections)
    before = lax.rem(seg + sections - 1, sections)
    batch, sec = part.shape[1:]
    height = batch // chunks
    groups = height // 8
    blocks = peers // groups
    lanes = sec // blocks

    barrier = pltpu.get_barrier_semaphore()
    for k in range(1, peers):
        pl.semaphore_signal(
            barrier, inc=1, device_id={"row": lax.rem(row + k, peers)}, device_id_type=MESH
        )
    for other in (after, before):
        pl.semaphore_signal(barrier, inc=1, device_id={"segment": other}, device_id_type=MESH)

    far = sorted(range(1, peers), key=lambda k: min(k, peers - k))

    def place(c, owner):
        top = pl.multiple_of(c * height + (owner // blocks) * 8, 8)
        left = pl.multiple_of(lax.rem(owner, blocks) * lanes, lanes)
        return pl.ds(top, 8), pl.ds(left, lanes)

    def take(p, c, sem):
        span = inbox.at[p, c, pl.ds(1, peers - 1)]
        pltpu.make_async_copy(span, span, sem).wait()

    v_load.wait()
    vt[...] = v_ref[...].T
    q_load.wait()
    high, low = split(q_ref[...])
    qh[...] = high
    ql[...] = low

    q_copy = pltpu.make_async_remote_copy(
        src_ref=q_ref, dst_ref=q2, send_sem=q_sem.at[0], recv_sem=q_sem.at[1],
        device_id={"segment": before}, device_id_type=MESH,
    )

    for p in range(2 * TICKS):
        now = (qh, ql) if p < 2 else (q2h, q2l)
        prior = (qh, ql) if p - 1 < 2 else (q2h, q2l)
        for c in range(chunks):
            span = pl.ds(c * height, height)
            if p > 0:
                take(p - 1, c, ag_recv.at[p - 1, c])
                vec = vt[span, :] - product(full[p - 1, span, :], *prior, NT)
                vt[span, :] = vec
            else:
                vec = vt[span, :]
            part[p, span, :] = product(vec, *now, NN)
            if p == 0 and c == 0:
                pl.semaphore_wait(barrier, peers + 1)
            for k in far:
                peer = lax.rem(row + k, peers)
                pltpu.make_async_remote_copy(
                    src_ref=part.at[(p,) + place(c, peer)],
                    dst_ref=inbox.at[p, c, k],
                    send_sem=rs_send.at[p, c], recv_sem=rs_recv.at[p, c],
                    device_id={"row": peer}, device_id_type=MESH,
                ).start()
        if p == 0:
            q_copy.start()
        if p == 2:
            here_ref[...] = (full[0] + full[1]).T
        for c in range(chunks):
            own = (p,) + place(c, row)
            take(p, c, rs_recv.at[p, c])
            total = part[own]
            for k in range(1, peers):
                total = total + inbox[p, c, k]
            mine[p, c] = total
            full[own] = total
            for k in far:
                pltpu.make_async_remote_copy(
                    src_ref=mine.at[p, c], dst_ref=full.at[own],
                    send_sem=ag_send.at[p, c], recv_sem=ag_recv.at[p, c],
                    device_id={"row": lax.rem(row + k, peers)}, device_id_type=MESH,
                ).start()
        if p == 1:
            q_copy.wait()
            high, low = split(q2[...])
            q2h[...] = high
            q2l[...] = low

    moves = []
    for c in range(chunks):
        span = pl.ds(c * height, height)
        take(3, c, ag_recv.at[3, c])
        csend[span, :] = full[2, span, :] + full[3, span, :]
        move = pltpu.make_async_remote_copy(
            src_ref=csend.at[span], dst_ref=cin.at[span],
            send_sem=c_send.at[c], recv_sem=c_recv.at[c],
            device_id={"segment": after}, device_id_type=MESH,
        )
        move.start()
        moves.append(move)
        vt[span, :] = vt[span, :] - product(full[3, span, :], q2h, q2l, NT)
    res = vt[...].T
    sums = jnp.sum(res * res, axis=0, keepdims=True)
    ssend[...] = jnp.broadcast_to(sums, ssend.shape)
    for k in far:
        pltpu.make_async_remote_copy(
            src_ref=ssend, dst_ref=sin.at[k], send_sem=s_send, recv_sem=s_recv,
            device_id={"row": lax.rem(row + k, peers)}, device_id_type=MESH,
        ).start()
    res_ref[...] = res
    for p in range(2 * TICKS):
        for c in range(chunks):
            take(p, c, rs_send.at[p, c])
            take(p, c, ag_send.at[p, c])
    for move in moves:
        move.wait()
    there_ref[...] = cin[...].T
    some = sin.at[pl.ds(1, peers - 1)]
    pltpu.make_async_copy(some, some, s_recv).wait()
    total = ssend[...]
    for k in range(1, peers):
        total = total + sin[k]
    sums_ref[...] = total
    pltpu.make_async_copy(some, some, s_send).wait()


def finish(sections, total_rows, res_ref, here_ref, there_ref, sums_ref, out_ref, coef_ref, rms_ref):
    seg = lax.axis_index("segment")
    batch = here_ref.shape[1]
    out_ref[...] = res_ref[...]
    rms_ref[...] = jnp.sqrt(sums_ref[...][:1] / total_rows)
    coef_ref[...] = jnp.zeros_like(coef_ref)
    before = lax.rem(seg + sections - 1, sections)
    coef_ref[:, pl.ds(pl.multiple_of(seg * batch, batch), batch)] = here_ref[...]
    coef_ref[:, pl.ds(pl.multiple_of(before * batch, batch), batch)] = there_ref[...]


def per_device(snapshots, basis):
    sections = lax.axis_size("segment")
    peers = lax.axis_size("row")
    rows, batch = snapshots.shape
    sec = basis.shape[1]
    chunks = max(1, min(CHUNKS, batch * sec // (8 * 128 * peers)))
    height = batch // chunks
    lanes = sec // (peers // (height // 8))
    phases = 2 * TICKS
    f32, bf16 = jnp.float32, jnp.bfloat16
    vmem = pl.BlockSpec(memory_space=pltpu.VMEM)
    dma = pltpu.SemaphoreType.DMA
    anywhere = pl.BlockSpec(memory_space=pl.ANY)
    parts = pl.pallas_call(
        functools.partial(kernel, peers, sections, chunks),
        out_shape=(
            pltpu.VMEM((rows, batch), f32),
            pltpu.VMEM((sec, batch), f32),
            pltpu.VMEM((sec, batch), f32),
            pltpu.VMEM((8, batch), f32),
        ),
        in_specs=[anywhere, anywhere],
        out_specs=(vmem, vmem, vmem, vmem),
        scratch_shapes=[
            pltpu.VMEM((rows, batch), f32),
            pltpu.VMEM((rows, sec), f32),
            dma((2,)),
            pltpu.VMEM((batch, rows), f32),
            pltpu.VMEM((rows, sec), bf16),
            pltpu.VMEM((rows, sec), bf16),
            pltpu.VMEM((rows, sec), f32),
            pltpu.VMEM((rows, sec), bf16),
            pltpu.VMEM((rows, sec), bf16),
            pltpu.VMEM((phases, batch, sec), f32),
            pltpu.VMEM((phases, chunks, peers, 8, lanes), f32),
            pltpu.VMEM((phases, chunks, 8, lanes), f32),
            pltpu.VMEM((phases, batch, sec), f32),
            pltpu.VMEM((batch, sec), f32),
            pltpu.VMEM((batch, sec), f32),
            pltpu.VMEM((8, batch), f32),
            pltpu.VMEM((peers, 8, batch), f32),
            dma((phases, chunks)),
            dma((phases, chunks)),
            dma((phases, chunks)),
            dma((phases, chunks)),
            dma((2,)),
            dma((chunks,)),
            dma((chunks,)),
            dma,
            dma,
        ],
        compiler_params=pltpu.CompilerParams(collective_id=0, has_side_effects=True),
    )(snapshots, basis)
    res, coef, rms = pl.pallas_call(
        functools.partial(finish, sections, rows * peers),
        out_shape=(
            jax.ShapeDtypeStruct((rows, batch), f32),
            jax.ShapeDtypeStruct((sec, batch * sections), f32),
            jax.ShapeDtypeStruct((1, batch), f32),
        ),
        in_specs=[vmem] * 4,
        out_specs=(vmem, vmem, vmem),
    )(*[pltpu.with_memory_space_constraint(p, pltpu.VMEM) for p in parts])
    return (res, coef, rms.reshape(batch))


CHUNKS = 4


def solution(mesh):
    placed = (P("row", "segment"), P("row", "segment"))
    return jax.shard_map(
        per_device,
        mesh=mesh,
        in_specs=placed,
        out_specs=(P("row", "segment"), P("segment", None), P("segment")),
        check_vma=False,
    )
```

```python
import functools

import jax
import jax.numpy as jnp
from jax import lax
from jax.experimental import pallas as pl
from jax.experimental.pallas import tpu as pltpu
from jax.sharding import PartitionSpec as P

TICKS = 2
MESH = pl.DeviceIdType.MESH
NN = (((1,), (0,)), ((), ()))
NT = (((1,), (1,)), ((), ()))


def split(x):
    high = x.astype(jnp.bfloat16)
    return high, (x - high.astype(jnp.float32)).astype(jnp.bfloat16)


def product(a, high_ref, low_ref, dims):
    rows = a.shape[0]
    high, low = split(a)
    both = lax.dot_general(
        jnp.concatenate([high, low], axis=0), high_ref[...], dims,
        preferred_element_type=jnp.float32,
    )
    rest = lax.dot_general(high, low_ref[...], dims, preferred_element_type=jnp.float32)
    return both[:rows] + (both[rows:] + rest)


def kernel(
    peers, sections, chunks,
    v_hbm, q_hbm, res_ref, here_ref, there_ref, sums_ref,
    v_ref, q_ref, in_sem,
    vt, qh, ql, q2, q2h, q2l, part, inbox, mine, full, csend, cin, ssend, sin,
    rs_send, rs_recv, ag_send, ag_recv, q_sem, c_send, c_recv, s_send, s_recv,
):
    q_load = pltpu.make_async_copy(q_hbm, q_ref, in_sem.at[0])
    v_load = pltpu.make_async_copy(v_hbm, v_ref, in_sem.at[1])
    q_load.start()
    v_load.start()
    row = lax.axis_index("row")
    seg = lax.axis_index("segment")
    after = lax.rem(seg + 1, sections)
    before = lax.rem(seg + sections - 1, sections)
    batch, sec = part.shape[1:]
    height = batch // chunks
    groups = height // 8
    blocks = peers // groups
    lanes = sec // blocks

    barrier = pltpu.get_barrier_semaphore()
    for k in range(1, peers):
        pl.semaphore_signal(
            barrier, inc=1, device_id={"row": lax.rem(row + k, peers)}, device_id_type=MESH
        )
    for other in (after, before):
        pl.semaphore_signal(barrier, inc=1, device_id={"segment": other}, device_id_type=MESH)

    far = sorted(range(1, peers), key=lambda k: min(k, peers - k))

    def place(c, owner):
        top = pl.multiple_of(c * height + (owner // blocks) * 8, 8)
        left = pl.multiple_of(lax.rem(owner, blocks) * lanes, lanes)
        return pl.ds(top, 8), pl.ds(left, lanes)

    def take(p, c, sem):
        span = inbox.at[p, c, pl.ds(1, peers - 1)]
        pltpu.make_async_copy(span, span, sem).wait()

    v_load.wait()
    vt[...] = v_ref[...].T
    q_load.wait()
    high, low = split(q_ref[...])
    qh[...] = high
    ql[...] = low

    q_copy = pltpu.make_async_remote_copy(
        src_ref=q_ref, dst_ref=q2, send_sem=q_sem.at[0], recv_sem=q_sem.at[1],
        device_id={"segment": before}, device_id_type=MESH,
    )

    for p in range(2 * TICKS):
        now = (qh, ql) if p < 2 else (q2h, q2l)
        prior = (qh, ql) if p - 1 < 2 else (q2h, q2l)
        for c in range(chunks):
            span = pl.ds(c * height, height)
            if p > 0:
                take(p - 1, c, ag_recv.at[p - 1, c])
                vec = vt[span, :] - product(full[p - 1, span, :], *prior, NT)
                vt[span, :] = vec
            else:
                vec = vt[span, :]
            part[p, span, :] = product(vec, *now, NN)
            if p == 0 and c == 0:
                pl.semaphore_wait(barrier, peers + 1)
            for k in far:
                peer = lax.rem(row + k, peers)
                pltpu.make_async_remote_copy(
                    src_ref=part.at[(p,) + place(c, peer)],
                    dst_ref=inbox.at[p, c, k],
                    send_sem=rs_send.at[p, c], recv_sem=rs_recv.at[p, c],
                    device_id={"row": peer}, device_id_type=MESH,
                ).start()
        if p == 0:
            q_copy.start()
        if p == 2:
            here_ref[...] = (full[0] + full[1]).T
        for c in range(chunks):
            own = (p,) + place(c, row)
            take(p, c, rs_recv.at[p, c])
            total = part[own]
            for k in range(1, peers):
                total = total + inbox[p, c, k]
            mine[p, c] = total
            full[own] = total
            for k in far:
                pltpu.make_async_remote_copy(
                    src_ref=mine.at[p, c], dst_ref=full.at[own],
                    send_sem=ag_send.at[p, c], recv_sem=ag_recv.at[p, c],
                    device_id={"row": lax.rem(row + k, peers)}, device_id_type=MESH,
                ).start()
        if p == 1:
            q_copy.wait()
            high, low = split(q2[...])
            q2h[...] = high
            q2l[...] = low

    moves = []
    for c in range(chunks):
        span = pl.ds(c * height, height)
        take(3, c, ag_recv.at[3, c])
        csend[span, :] = full[2, span, :] + full[3, span, :]
        move = pltpu.make_async_remote_copy(
            src_ref=csend.at[span], dst_ref=cin.at[span],
            send_sem=c_send.at[c], recv_sem=c_recv.at[c],
            device_id={"segment": after}, device_id_type=MESH,
        )
        move.start()
        moves.append(move)
    res = (vt[...] - product(full[3], q2h, q2l, NT)).T
    sums = jnp.sum(res * res, axis=0, keepdims=True)
    ssend[...] = jnp.broadcast_to(sums, ssend.shape)
    for k in far:
        pltpu.make_async_remote_copy(
            src_ref=ssend, dst_ref=sin.at[k], send_sem=s_send, recv_sem=s_recv,
            device_id={"row": lax.rem(row + k, peers)}, device_id_type=MESH,
        ).start()
    res_ref[...] = res
    for p in range(2 * TICKS):
        for c in range(chunks):
            take(p, c, rs_send.at[p, c])
            take(p, c, ag_send.at[p, c])
    for move in moves:
        move.wait()
    there_ref[...] = cin[...].T
    some = sin.at[pl.ds(1, peers - 1)]
    pltpu.make_async_copy(some, some, s_recv).wait()
    total = ssend[...]
    for k in range(1, peers):
        total = total + sin[k]
    sums_ref[...] = total
    pltpu.make_async_copy(some, some, s_send).wait()


def finish(sections, total_rows, res_ref, here_ref, there_ref, sums_ref, out_ref, coef_ref, rms_ref):
    seg = lax.axis_index("segment")
    batch = here_ref.shape[1]
    out_ref[...] = res_ref[...]
    rms_ref[...] = jnp.sqrt(sums_ref[...][:1] / total_rows)
    coef_ref[...] = jnp.zeros_like(coef_ref)
    before = lax.rem(seg + sections - 1, sections)
    coef_ref[:, pl.ds(pl.multiple_of(seg * batch, batch), batch)] = here_ref[...]
    coef_ref[:, pl.ds(pl.multiple_of(before * batch, batch), batch)] = there_ref[...]


def per_device(snapshots, basis):
    sections = lax.axis_size("segment")
    peers = lax.axis_size("row")
    rows, batch = snapshots.shape
    sec = basis.shape[1]
    chunks = max(1, min(CHUNKS, batch * sec // (8 * 128 * peers)))
    height = batch // chunks
    lanes = sec // (peers // (height // 8))
    phases = 2 * TICKS
    f32, bf16 = jnp.float32, jnp.bfloat16
    vmem = pl.BlockSpec(memory_space=pltpu.VMEM)
    dma = pltpu.SemaphoreType.DMA
    anywhere = pl.BlockSpec(memory_space=pl.ANY)
    parts = pl.pallas_call(
        functools.partial(kernel, peers, sections, chunks),
        out_shape=(
            pltpu.VMEM((rows, batch), f32),
            pltpu.VMEM((sec, batch), f32),
            pltpu.VMEM((sec, batch), f32),
            pltpu.VMEM((8, batch), f32),
        ),
        in_specs=[anywhere, anywhere],
        out_specs=(vmem, vmem, vmem, vmem),
        scratch_shapes=[
            pltpu.VMEM((rows, batch), f32),
            pltpu.VMEM((rows, sec), f32),
            dma((2,)),
            pltpu.VMEM((batch, rows), f32),
            pltpu.VMEM((rows, sec), bf16),
            pltpu.VMEM((rows, sec), bf16),
            pltpu.VMEM((rows, sec), f32),
            pltpu.VMEM((rows, sec), bf16),
            pltpu.VMEM((rows, sec), bf16),
            pltpu.VMEM((phases, batch, sec), f32),
            pltpu.VMEM((phases, chunks, peers, 8, lanes), f32),
            pltpu.VMEM((phases, chunks, 8, lanes), f32),
            pltpu.VMEM((phases, batch, sec), f32),
            pltpu.VMEM((batch, sec), f32),
            pltpu.VMEM((batch, sec), f32),
            pltpu.VMEM((8, batch), f32),
            pltpu.VMEM((peers, 8, batch), f32),
            dma((phases, chunks)),
            dma((phases, chunks)),
            dma((phases, chunks)),
            dma((phases, chunks)),
            dma((2,)),
            dma((chunks,)),
            dma((chunks,)),
            dma,
            dma,
        ],
        compiler_params=pltpu.CompilerParams(collective_id=0, has_side_effects=True),
    )(snapshots, basis)
    res, coef, rms = pl.pallas_call(
        functools.partial(finish, sections, rows * peers),
        out_shape=(
            jax.ShapeDtypeStruct((rows, batch), f32),
            jax.ShapeDtypeStruct((sec, batch * sections), f32),
            jax.ShapeDtypeStruct((1, batch), f32),
        ),
        in_specs=[vmem] * 4,
        out_specs=(vmem, vmem, vmem),
    )(*[pltpu.with_memory_space_constraint(p, pltpu.VMEM) for p in parts])
    return (res, coef, rms.reshape(batch))


CHUNKS = 4


def solution(mesh):
    placed = (P("row", "segment"), P("row", "segment"))
    return jax.shard_map(
        per_device,
        mesh=mesh,
        in_specs=placed,
        out_specs=(P("row", "segment"), P("segment", None), P("segment")),
        check_vma=False,
    )
```
